32 devices in a mesh: ctx: 8 (over z, x), tp: 4 (over y, core).
Axes of the slice: x: 2, y: 2, z: 4, core: 2. Of those that a mesh axis runs over, the one named last changes fastest.
Arguments:
- tokens: bfloat16 [4096, 4096], P(('ctx', 'tp')), may hold values from -6 to 6
- in_weight: bfloat16 [4096, 3, 4096], P('ctx', None, 'tp'), may hold values from -0.09375 to 0.09375
- short_filter: float32 [3, 3, 4096], P(None, None, 'tp'), may hold values from -3 to 3
- decay_rates: float32 [16, 4096], P(None, 'tp'), may hold values from 1.2207031e-05 to 0.1, as said below
- residues: float32 [16, 4096], P(None, 'tp'), may hold values from -1.5 to 1.5
- skip_gain: float32 [4096], P('tp'), may hold values from -4 to 4
Outputs:
- mixed: bfloat16 [4096, 4096], P('ctx', 'tp')
The draws below stay inside these ranges and needn't reach their ends.
Inputs may be any that keep to these rules, and one draw needn't show every extreme that they name: `decay_rates`: positive decay rates.
All inputs are finite; a program needn't handle non-finite values.
Results may differ from the reference program's by a relative error of at most 0.0063.
Values may be sent and summed in bfloat16 or wider, within the bound.
A program may use at most 128 MiB of HBM per device.

```python
import jax
import jax.numpy as jnp
from jax import lax

D = 4096
MODES = 16
SHORT = 3
BLOCK = 32
SEQ = 4096


def draw_decay_rates(key, part):
    first, second, third = jax.random.split(key, 3)
    share = 0.5
    pick_slow = jax.random.uniform(first, (MODES, D), jnp.float32) < share
    slow_rates = jnp.exp(jax.random.uniform(second, (MODES, D), jnp.float32, jnp.log(0.05 / SEQ), jnp.log(2.0 / SEQ)))
    fast_rates = jnp.exp(jax.random.uniform(third, (MODES, D), jnp.float32, jnp.log(1.0 / 50.0), jnp.log(0.1)))
    return jnp.where(pick_slow, slow_rates, fast_rates).astype(jnp.float32)


def block_scale(rng, shape, shards, smallest, largest):
    gain = 1.0
    for position, shards_of in shards:
        steps = jax.random.uniform(jax.random.fold_in(jax.random.fold_in(rng, 6), position), (shards_of,), jnp.float32, smallest / len(shards), largest / len(shards))
        gain = gain * jnp.repeat(jnp.exp(steps), shape[position] // shards_of).reshape((-1,) + (1,) * (len(shape) - 1 - position))
    return gain


def scatter_about(stream_key, extent, width, bound, cuts=(), kind=jnp.bfloat16):
    array = jax.random.normal(stream_key, extent, jnp.float32) * width
    if len(cuts) > 0:
        array = block_scale(stream_key, extent, cuts, -0.22, 0.18) * array
    return jnp.clip(array, min=-bound, max=bound).astype(kind)


def setup_inputs(seed: int = 0) -> dict:
    arg_keys = jax.random.split(jax.random.key(seed), 7)
    return {
        "tokens": scatter_about(arg_keys[0], (SEQ, D), 1.0, 6.0, ((0, 32),)),
        "in_weight": scatter_about(arg_keys[1], (D, 3, D), D ** -0.5, 0.09375, ((0, 8), (2, 4))),
        "short_filter": scatter_about(arg_keys[2], (3, SHORT, D), 0.6, 3.0, ((2, 4),), jnp.float32),
        "decay_rates": draw_decay_rates(jax.random.fold_in(arg_keys[6], 71), 0),
        "residues": scatter_about(arg_keys[4], (MODES, D), 0.25, 1.5, ((1, 4),), jnp.float32),
        "skip_gain": scatter_about(arg_keys[5], (D,), 1.0, 4.0, ((0, 4),), jnp.float32),
    }


def block_scan(product, decay_rates, residues, block):
    channels = product.shape[1]
    mode_gain = residues * jnp.sqrt(2.0 * decay_rates)
    positions = jnp.arange(block, dtype=jnp.float32)
    kernel = lax.optimization_barrier(jnp.sum(mode_gain[None] * jnp.exp(-decay_rates[None] * positions[:, None, None]), axis=1))
    gaps = jnp.arange(block, dtype=jnp.int32)[:, None] - jnp.arange(block, dtype=jnp.int32)[None, :]
    toeplitz = jnp.where((gaps >= 0)[:, :, None], kernel[jnp.clip(gaps, 0, block - 1)], jnp.float32(0.0))
    read_out = mode_gain[None] * jnp.exp(-decay_rates[None] * (positions[:, None, None] + 1.0))
    take_in = jnp.exp(-decay_rates[None] * (block - 1.0 - positions)[:, None, None])
    step_decay = jnp.exp(-decay_rates * block)

    def advance(state, block_in):
        block_out = lax.optimization_barrier(jnp.sum(toeplitz * block_in[None], axis=1)) + lax.optimization_barrier(jnp.sum(read_out * state[None], axis=1))
        state = step_decay * state + lax.optimization_barrier(jnp.sum(take_in * block_in[:, None, :], axis=0))
        return (state, block_out)
    zero_state = jnp.zeros(decay_rates.shape, jnp.float32)
    state, outputs = lax.scan(advance, zero_state, product.reshape(-1, block, channels))
    return (outputs.reshape(-1, channels), state)

def reference(tokens, in_weight, short_filter, decay_rates, residues, skip_gain):
    projected = jnp.dot(tokens, in_weight.reshape(D, 3 * D), preferred_element_type=jnp.float32)
    projected = projected.astype(jnp.bfloat16).reshape(SEQ, 3, D)
    widened = jnp.pad(projected.astype(jnp.float32), ((SHORT - 1, 0), (0, 0), (0, 0)))
    features = jnp.zeros((SEQ, 3, D), jnp.float32)
    for offset in range(SHORT):
        features = features + short_filter[None, :, offset, :] * widened[SHORT - 1 - offset:SHORT - 1 - offset + SEQ]
    product = features[:, 1] * features[:, 2]
    inside, state = block_scan(product, decay_rates, residues, BLOCK)
    return (features[:, 0] * (inside + skip_gain[None] * product)).astype(jnp.bfloat16)
```

```python
import functools

import jax
import jax.numpy as jnp
from jax import lax
from jax.experimental import pallas as pl
from jax.experimental.pallas import tpu as pltpu
from jax.sharding import PartitionSpec as P

MESH = pl.DeviceIdType.MESH
VMEM_BYTES = 60 * 1024 * 1024
SUBLANES = 8
TAIL = 16
LANES = 128


def flipped(index, bit):
    return index + bit - 2 * bit * ((index // bit) % 2)


def gather_kernel(Z, X, T, tok_ref, w_ref, out_ref, tok, w, tok_recv, w_recv, send_z, send_t, send_wz, send_wx, own_sem):
    ctx, t = lax.axis_index("ctx"), lax.axis_index("tp")
    z, x = ctx // X, ctx % X
    bits = []
    bit = T // 2
    while bit:
        bits.append(bit)
        bit //= 2

    own_tok = pltpu.make_async_copy(tok_ref, tok.at[z, t], own_sem.at[0])
    own_w = pltpu.make_async_copy(w_ref.at[z], w.at[z, x], own_sem.at[1])
    own_tok.start()
    own_w.start()

    barrier = pltpu.get_barrier_semaphore()
    for o in range(1, Z):
        pl.semaphore_signal(barrier, inc=1, device_id=(((z + o) % Z) * X + x, t), device_id_type=MESH)
    for o in range(1, X):
        pl.semaphore_signal(barrier, inc=1, device_id=(z * X + (x + o) % X, t), device_id_type=MESH)
    for bit in bits:
        pl.semaphore_signal(barrier, inc=1, device_id=(ctx, flipped(t, bit)), device_id_type=MESH)
    pl.semaphore_wait(barrier, Z - 1 + X - 1 + len(bits))

    def remote(src, dst, send, recv, device):
        return pltpu.make_async_remote_copy(
            src_ref=src, dst_ref=dst, send_sem=send, recv_sem=recv, device_id=device, device_id_type=MESH
        )

    def tok_line(side, source, src):
        to = z + 1 if side == 0 else z - 1
        return remote(
            src, tok.at[source, t], send_z.at[side, source], tok_recv.at[source, t], (to * X + x, t)
        )

    def exists(side, s):
        return z - s >= 0 if side == 0 else z + s < Z

    def held(level):
        masks = [0]
        for bit in bits[:level]:
            masks = masks + [m + bit for m in masks]
        return masks

    def slot(mask):
        index = t
        for bit in bits:
            if mask & bit:
                index = flipped(index, bit)
        return index

    def tp_copies(level, source, own):
        copies = []
        for mask in held(level):
            q = slot(mask)
            src = tok_ref if own and mask == 0 else tok.at[source, q]
            copies.append(
                remote(
                    src,
                    tok.at[source, q],
                    send_t.at[level, source, mask],
                    tok_recv.at[source, q],
                    (ctx, flipped(t, bits[level])),
                )
            )
        return copies

    def tok_arrived(source, q):
        remote(tok.at[source, q], tok.at[source, q], own_sem.at[0], tok_recv.at[source, q], (ctx, t)).wait_recv()

    def w_line(target):
        return remote(w_ref.at[target], w.at[z, x], send_wz.at[target], w_recv.at[z, x], (target * X + x, t))

    def w_cross(source, o, src):
        return remote(
            src, w.at[source, x], send_wx.at[source, o], w_recv.at[source, x], (z * X + (x + o) % X, t)
        )

    def w_arrived(source, q):
        remote(w.at[source, q], w.at[source, q], own_sem.at[0], w_recv.at[source, q], (ctx, t)).wait_recv()

    def multiply(source):
        depth = w.shape[0] * w.shape[1] * w.shape[2]
        rows = tok.shape[1] * tok.shape[2]
        a = tok.at[source].reshape(rows, depth)
        b = w.reshape(depth, w.shape[3])
        tile = 256 if w.shape[3] % 256 == 0 else 128

        @pl.loop(0, w.shape[3] // tile)
        def _(n):
            cols = pl.ds(pl.multiple_of(n * tile, tile), tile)
            out_ref[source, :, cols] = jnp.dot(
                a[...], b[:, cols], preferred_element_type=jnp.float32
            ).astype(out_ref.dtype)

    for side in (0, 1):
        @pl.when(z + 1 < Z if side == 0 else z >= 1)
        def _():
            tok_line(side, z, tok_ref).start()
    for o in range(1, X):
        w_cross(z, o, w_ref.at[z]).start()
    for s in range(Z - 1, 0, -1):
        for side in (0, 1):
            @pl.when(z + s < Z if side == 0 else z >= s)
            def _():
                w_line(z + s if side == 0 else z - s).start()

    def start_level(level, s):
        for side in (0, 1):
            if s == 0 and side == 1:
                continue

            def act():
                source = z - s if side == 0 else z + s
                if level > 0:
                    for mask in held(level - 1):
                        tok_arrived(source, slot(mask + bits[level - 1]))
                for copy in tp_copies(level, source, s == 0):
                    copy.start()

            if s == 0:
                act()
            else:
                pl.when(exists(side, s))(act)

    def take_line(s):
        for side in (0, 1):
            @pl.when(exists(side, s))
            def _():
                source = z - s if side == 0 else z + s
                tok_arrived(source, t)

                @pl.when(z + 1 < Z if side == 0 else z >= 1)
                def _():
                    tok_line(side, source, tok.at[source, t]).start()

    def finish(s):
        for side in (0, 1):
            if s == 0 and side == 1:
                continue

            def act():
                source = z - s if side == 0 else z + s
                for mask in held(len(bits) - 1):
                    tok_arrived(source, slot(mask + bits[-1]))
                multiply(source)

            if s == 0:
                act()
            else:
                pl.when(exists(side, s))(act)

    def take_w(s):
        for side in (0, 1):
            @pl.when(exists(side, s))
            def _():
                source = z - s if side == 0 else z + s
                w_arrived(source, x)
                for o in range(1, X):
                    w_cross(source, o, w.at[source, x]).start()

    start_level(0, 0)
    take_line(1)
    start_level(0, 1)
    for level in range(1, len(bits)):
        start_level(level, 0)
        start_level(level, 1)
    for s in range(Z - 1, 0, -1):
        take_w(s)
    own_tok.wait()
    own_w.wait()
    if Z > 2:
        take_line(2)
        start_level(0, 2)
    for source in range(Z):
        for o in range(1, X):
            w_arrived(source, (x + o) % X)
    finish(0)
    finish(1)
    for s in range(2, Z):
        if s > 2:
            take_line(s)
            start_level(0, s)
        for level in range(1, len(bits)):
            start_level(level, s)
        finish(s)

    for side in (0, 1):
        for s in range(Z - 1):
            @pl.when(jnp.logical_and(exists(side, s), z + 1 < Z if side == 0 else z >= 1))
            def _():
                source = z - s if side == 0 else z + s
                tok_line(side, source, tok.at[source, t]).wait_send()
    for source in range(Z):
        for o in range(1, X):
            w_cross(source, o, w.at[source, x]).wait_send()
        for level in range(len(bits)):
            for copy in tp_copies(level, source, False):
                copy.wait_send()
    for o in range(1, Z):
        w_line((z + o) % Z).wait_send()


def conv_kernel(Z, X, proj_ref, filt_ref, dec_ref, res_ref, skip_ref, out_ref,
                halo, wid, prod, gate, consts, st, seg, allseg, outbuf,
                halo_sems, seg_send, seg_recv, out_send, out_recv, own_sem):
    ctx, t = lax.axis_index("ctx"), lax.axis_index("tp")
    z, x = ctx // X, ctx % X
    groups, L = prod.shape[1], prod.shape[2]
    C = groups * LANES
    modes = dec_ref.shape[0]
    lags = filt_ref.shape[0] // 3
    steps = L // SUBLANES
    lane0 = pl.multiple_of(z * C, LANES)
    cols = pl.ds(lane0, C)

    barrier = pltpu.get_barrier_semaphore()
    for o in range(1, Z):
        pl.semaphore_signal(barrier, inc=1, device_id=(((z + o) % Z) * X + x, t), device_id_type=MESH)
    for o in range(1, X):
        pl.semaphore_signal(barrier, inc=1, device_id=(z * X + (x + o) % X, t), device_id_type=MESH)
    pl.semaphore_wait(barrier, Z - 1 + X - 1)

    tails = pltpu.make_async_remote_copy(
        src_ref=proj_ref.at[:, pl.ds(L - TAIL, TAIL), :], dst_ref=halo,
        send_sem=halo_sems.at[0], recv_sem=halo_sems.at[1],
        device_id=(z * X + (x + 1) % X, t), device_id_type=MESH,
    )
    tails.start()

    dec = dec_ref[:, cols]
    gain = res_ref[:, cols] * jnp.sqrt(2.0 * dec)
    decay = jnp.exp(-dec)
    sub_decay = jnp.exp(-dec * steps)
    seg_decay = jnp.exp(-dec * L)
    for m in range(modes):
        consts[0, m] = jnp.broadcast_to(decay[m : m + 1], (SUBLANES, C))
        consts[1, m] = jnp.broadcast_to(gain[m : m + 1], (SUBLANES, C))
    skip = skip_ref[:, cols]
    filt = filt_ref[:, cols]
    tails.wait()

    rows = 32

    @pl.loop(0, Z)
    def _(s):
        before = jnp.where(x == 0, s - 1, s)
        tail = halo[jnp.maximum(before, 0)].astype(jnp.float32)
        wid[0:SUBLANES] = jnp.where(before >= 0, tail[TAIL - SUBLANES :], 0.0)
        wid[SUBLANES:] = proj_ref[s].astype(jnp.float32)

        @pl.loop(0, L // rows)
        def _(r):
            start = pl.multiple_of(r * rows, rows)
            feats = []
            for j in range(3):
                block = wid[pl.ds(start, rows + SUBLANES), j * C : (j + 1) * C]
                total = None
                for o in range(lags):
                    term = filt[j * lags + o][None] * block[SUBLANES - o : SUBLANES - o + rows]
                    total = term if total is None else total + term
                feats.append(total)
            value = feats[1] * feats[2]
            for g in range(groups):
                lanes = slice(g * LANES, (g + 1) * LANES)
                gate[s, g, pl.ds(start, rows), :] = feats[0][:, lanes]
                prod[s, g, pl.ds(start, rows), :] = value[:, lanes]

    @pl.loop(0, Z)
    def _(s):
        for g in range(groups):
            lanes = slice(g * LANES, (g + 1) * LANES)
            factor = [consts[0, m, :, lanes] for m in range(modes)]

            def step(i, state):
                v = prod[s, g, pl.ds(i, SUBLANES, stride=steps), :]
                return tuple(f * q + v for f, q in zip(factor, state))

            zero = jnp.zeros((SUBLANES, LANES), jnp.float32)
            state = lax.fori_loop(0, steps, step, (zero,) * modes, unroll=4)
            for m in range(modes):
                st[s, m, :, lanes] = state[m]
        e = jnp.zeros((modes, C), jnp.float32)
        for c in range(SUBLANES):
            e = sub_decay * e + st[s, :, c, :]
        seg[s] = e

    allseg[x] = seg[...]
    sends = []
    for o in range(1, X):
        sends.append(pltpu.make_async_remote_copy(
            src_ref=seg, dst_ref=allseg.at[x], send_sem=seg_send.at[o], recv_sem=seg_recv.at[x],
            device_id=(z * X + (x + o) % X, t), device_id_type=MESH,
        ))
        sends[-1].start()
    for o in range(1, X):
        q = (x + o) % X
        pltpu.make_async_remote_copy(
            src_ref=seg, dst_ref=allseg.at[q], send_sem=seg_send.at[o], recv_sem=seg_recv.at[q],
            device_id=(z * X + q, t), device_id_type=MESH,
        ).wait_recv()
    for copy in sends:
        copy.wait_send()

    carry = jnp.zeros((modes, C), jnp.float32)
    for s in range(Z):
        mine = jnp.zeros((modes, C), jnp.float32)
        for q in range(X):
            mine = jnp.where(x == q, carry, mine)
            carry = seg_decay * carry + allseg[q, s]
        seg[s] = mine

    def out_copy(s):
        return pltpu.make_async_remote_copy(
            src_ref=outbuf.at[s], dst_ref=out_ref.at[:, cols], send_sem=out_send.at[s], recv_sem=out_recv.at[z],
            device_id=(s * X + x, t), device_id_type=MESH,
        )

    own_out = pltpu.make_async_copy(outbuf.at[z], out_ref.at[:, cols], own_sem)

    @pl.loop(0, Z)
    def _(k):
        s = (z + 1 + k) % Z
        e = seg[s]
        for c in range(SUBLANES):
            now = st[s, :, c, :]
            st[s, :, c, :] = e
            e = sub_decay * e + now
        for g in range(groups):
            lanes = slice(g * LANES, (g + 1) * LANES)
            direct = jnp.broadcast_to(skip[:, lanes], (SUBLANES, LANES))

            def step(i, state):
                at = pl.ds(i, SUBLANES, stride=steps)
                v = prod[s, g, at, :]
                state = tuple(consts[0, m, :, lanes] * q + v for m, q in enumerate(state))
                parts = [consts[1, m, :, lanes] * q for m, q in enumerate(state)]
                parts.append(direct * v)
                while len(parts) > 1:
                    parts = [a + b for a, b in zip(parts[::2], parts[1::2])] + (
                        [parts[-1]] if len(parts) % 2 else []
                    )
                gate[s, g, at, :] = gate[s, g, at, :] * parts[0]
                return state

            lax.fori_loop(0, steps, step, tuple(st[s, m, :, lanes] for m in range(modes)), unroll=4)
            outbuf[s, :, lanes] = gate[s, g].astype(outbuf.dtype)

        @pl.when(s != z)
        def _():
            out_copy(s).start()

        @pl.when(s == z)
        def _():
            own_out.start()

    own_out.wait()
    for o in range(1, Z):
        q = (z + o) % Z
        out_copy(q).wait_send()
        pltpu.make_async_remote_copy(
            src_ref=outbuf.at[q], dst_ref=out_ref.at[:, pl.ds(pl.multiple_of(q * C, LANES), C)],
            send_sem=out_send.at[q], recv_sem=out_recv.at[q],
            device_id=(q * X + x, t), device_id_type=MESH,
        ).wait_recv()


def line_length(count, token_bytes, weight_bytes, channels):
    best = None
    for Z in range(1, count):
        if count % Z or channels % (Z * LANES):
            continue
        cost = token_bytes * Z + 2 * weight_bytes // Z
        if best is None or cost < best[0]:
            best = (cost, Z)
    return best[1]


def per_device(tokens, in_weight, short_filter, decay_rates, residues, skip_gain):
    count, T = lax.axis_size("ctx"), lax.axis_size("tp")
    R, D = tokens.shape
    depth, branches, channels = in_weight.shape
    modes = decay_rates.shape[0]
    Z = line_length(count, R * T * D, depth * count * branches * channels, channels)
    X = count // Z
    C = channels // Z
    L = R * T
    levels = max(1, (T - 1).bit_length())
    wide = branches * C
    pieces = in_weight.reshape(depth, branches, Z, C).transpose(2, 0, 1, 3).reshape(Z, depth, wide)
    dma = pltpu.SemaphoreType.DMA
    hbm = pl.BlockSpec(memory_space=pl.ANY)
    vmem = pl.BlockSpec(memory_space=pltpu.VMEM)
    projected = pl.pallas_call(
        functools.partial(gather_kernel, Z, X, T),
        out_shape=jax.ShapeDtypeStruct((Z, L, wide), jnp.bfloat16),
        in_specs=[hbm, hbm],
        out_specs=vmem,
        scratch_shapes=[
            pltpu.VMEM((Z, T, R, D), jnp.bfloat16),
            pltpu.VMEM((Z, X, depth, wide), jnp.bfloat16),
            dma((Z, T)), dma((Z, X)), dma((2, Z)), dma((levels, Z, T)), dma((Z,)), dma((Z, X)), dma((2,)),
        ],
        compiler_params=pltpu.CompilerParams(
            collective_id=0, has_side_effects=True, vmem_limit_bytes=VMEM_BYTES
        ),
        name="gather_project",
    )(tokens, pieces)
    taps = short_filter.reshape(short_filter.shape[0] * short_filter.shape[1], channels)
    f32 = jnp.float32
    return pl.pallas_call(
        functools.partial(conv_kernel, Z, X),
        out_shape=jax.ShapeDtypeStruct((L, channels), jnp.bfloat16),
        in_specs=[vmem] * 5,
        out_specs=hbm,
        scratch_shapes=[
            pltpu.VMEM((Z, TAIL, wide), jnp.bfloat16),
            pltpu.VMEM((L + SUBLANES, wide), f32),
            pltpu.VMEM((Z, C // LANES, L, LANES), f32),
            pltpu.VMEM((Z, C // LANES, L, LANES), f32),
            pltpu.VMEM((2, modes, SUBLANES, C), f32),
            pltpu.VMEM((Z, modes, SUBLANES, C), f32),
            pltpu.VMEM((Z, modes, C), f32),
            pltpu.VMEM((X, Z, modes, C), f32),
            pltpu.VMEM((Z, L, C), jnp.bfloat16),
            dma((2,)), dma((X,)), dma((X,)), dma((Z,)), dma((Z,)), dma,
        ],
        compiler_params=pltpu.CompilerParams(
            collective_id=1, has_side_effects=True, vmem_limit_bytes=VMEM_BYTES
        ),
        name="short_long_filter",
    )(projected, taps, decay_rates, residues, skip_gain[None])


def solution(mesh):
    in_specs = (
        P(("ctx", "tp"), None),
        P("ctx", None, "tp"),
        P(None, None, "tp"),
        P(None, "tp"),
        P(None, "tp"),
        P("tp"),
    )
    return jax.shard_map(
        per_device, mesh=mesh, in_specs=in_specs, out_specs=P("ctx", "tp"), check_vma=False
    )
```

```python
import functools

import jax
import jax.numpy as jnp
from jax import lax
from jax.experimental import pallas as pl
from jax.experimental.pallas import tpu as pltpu
from jax.sharding import PartitionSpec as P

MESH = pl.DeviceIdType.MESH
VMEM_BYTES = 60 * 1024 * 1024
SUBLANES = 8
TAIL = 16
PIECES = 4
LANES = 128


def flipped(index, bit):
    return index + bit - 2 * bit * ((index // bit) % 2)


def fused_kernel(Z, X, T, tok_ref, w_ref, filt_ref, dec_ref, res_ref, skip_ref, out_ref,
                 tok, w, wid, tail, halo, prod, gate, consts, st, seg, allseg, outbuf,
                 tok_recv, w_recv, send_z, send_t, send_wz, send_wx,
                 halo_send, halo_recv, seg_send, seg_recv, out_send, out_recv, own_sem):
    ctx, t = lax.axis_index("ctx"), lax.axis_index("tp")
    z, x = ctx // X, ctx % X
    R = tok.shape[2]
    G = send_z.shape[2]
    part = R // G
    branches, depth = w.shape[0], w.shape[3]
    groups, L = prod.shape[1], prod.shape[2]
    C = groups * LANES
    modes, lags = dec_ref.shape[0], filt_ref.shape[1]
    steps = L // SUBLANES
    bits = []
    bit = T // 2
    while bit:
        bits.append(bit)
        bit //= 2

    def columns(index):
        return pl.ds(pl.multiple_of(index * C, LANES), C)

    own_tok = pltpu.make_async_copy(tok_ref, tok.at[z, t], own_sem.at[0])
    own_w = pltpu.make_async_copy(w_ref.at[:, :, columns(z)], w.at[:, z, x], own_sem.at[1])
    own_tok.start()
    own_w.start()

    barrier = pltpu.get_barrier_semaphore()
    for o in range(1, Z):
        pl.semaphore_signal(barrier, inc=1, device_id=(((z + o) % Z) * X + x, t), device_id_type=MESH)
    for o in range(1, X):
        pl.semaphore_signal(barrier, inc=1, device_id=(z * X + (x + o) % X, t), device_id_type=MESH)
    for bit in bits:
        pl.semaphore_signal(barrier, inc=1, device_id=(ctx, flipped(t, bit)), device_id_type=MESH)
    pl.semaphore_wait(barrier, Z - 1 + X - 1 + len(bits))

    def remote(src, dst, send, recv, device):
        return pltpu.make_async_remote_copy(
            src_ref=src, dst_ref=dst, send_sem=send, recv_sem=recv, device_id=device, device_id_type=MESH
        )

    def exists(side, s):
        return z - s >= 0 if side == 0 else z + s < Z

    def onward(side):
        return z + 1 < Z if side == 0 else z >= 1

    def at_distance(side, s):
        return z - s if side == 0 else z + s

    def piece(source, q, g):
        return tok.at[source, q, pl.ds(g * part, part)]

    def own_piece(g):
        return tok_ref.at[pl.ds(g * part, part)]

    def tok_line(side, source, g, src):
        to = z + 1 if side == 0 else z - 1
        return remote(
            src, piece(source, t, g), send_z.at[side, source, g], tok_recv.at[source, t, g], (to * X + x, t)
        )

    def held(level):
        masks = [0]
        for bit in bits[:level]:
            masks = masks + [m + bit for m in masks]
        return masks

    def slot(mask):
        index = t
        for bit in bits:
            if mask & bit:
                index = flipped(index, bit)
        return index

    def tp_copies(level, source, g, own):
        copies = []
        for mask in held(level):
            q = slot(mask)
            src = own_piece(g) if own and mask == 0 else piece(source, q, g)
            copies.append(
                remote(
                    src, piece(source, q, g), send_t.at[level, source, mask, g], tok_recv.at[source, q, g],
                    (ctx, flipped(t, bits[level])),
                )
            )
        return copies

    def tok_arrived(source, q, g):
        ref = piece(source, q, g)
        remote(ref, ref, own_sem.at[0], tok_recv.at[source, q, g], (ctx, t)).wait_recv()

    def w_line(target):
        return remote(
            w_ref.at[:, :, columns(target)], w.at[:, z, x], send_wz.at[target], w_recv.at[z, x], (target * X + x, t)
        )

    def w_cross(source, o, src):
        return remote(
            src, w.at[:, source, x], send_wx.at[source, o], w_recv.at[source, x], (z * X + (x + o) % X, t)
        )

    def w_arrived(source, q):
        ref = w.at[:, source, q]
        remote(ref, ref, own_sem.at[0], w_recv.at[source, q], (ctx, t)).wait_recv()

    def tail_copy(source):
        return remote(
            tail.at[source], halo.at[source], halo_send.at[source], halo_recv.at[source], (z * X + (x + 1) % X, t)
        )

    def seg_copy(source, o):
        return remote(
            seg.at[source], allseg.at[x, source], seg_send.at[source, o], seg_recv.at[x, source],
            (z * X + (x + o) % X, t),
        )

    def take_line(s, g):
        for side in (0, 1):
            @pl.when(exists(side, s))
            def _():
                source = at_distance(side, s)
                tok_arrived(source, t, g)

                @pl.when(onward(side))
                def _():
                    tok_line(side, source, g, piece(source, t, g)).start()

                if bits:
                    for copy in tp_copies(0, source, g, False):
                        copy.start()

    def start_level(level, s, g):
        for side in (0, 1) if s else (0,):
            def act():
                source = at_distance(side, s)
                if level > 0:
                    for mask in held(level - 1):
                        tok_arrived(source, slot(mask + bits[level - 1]), g)
                for copy in tp_copies(level, source, g, s == 0):
                    copy.start()

            pl.when(exists(side, s))(act)

    def take_w(s):
        for side in (0, 1):
            @pl.when(exists(side, s))
            def _():
                source = at_distance(side, s)
                w_arrived(source, x)
                for o in range(1, X):
                    w_cross(source, o, w.at[:, source, x]).start()

    def multiply(source):
        a = tok.at[source].reshape(T * R, Z * X * depth)

        @pl.loop(0, branches)
        def _(j):
            b = w.at[j].reshape(Z * X * depth, C)
            value = jnp.dot(a[...], b[...], preferred_element_type=jnp.float32).astype(jnp.bfloat16)
            tail[source, j] = value[L - TAIL :]
            wid[source, j, SUBLANES:] = value.astype(jnp.float32)

    rows = 32

    def local_filter(source):
        before = jnp.where(x == 0, source - 1, source)

        @pl.loop(0, branches)
        def _(j):
            last = halo[jnp.maximum(before, 0), j].astype(jnp.float32)
            wid[source, j, 0:SUBLANES] = jnp.where(before >= 0, last[TAIL - SUBLANES :], 0.0)

        @pl.loop(0, L // rows)
        def _(r):
            start = pl.multiple_of(r * rows, rows)
            feats = []
            for j in range(branches):
                block = wid[source, j, pl.ds(start, rows + SUBLANES)]
                total = None
                for o in range(lags):
                    term = filt_ref[j, o : o + 1, columns(z)] * block[SUBLANES - o : SUBLANES - o + rows]
                    total = term if total is None else total + term
                feats.append(total)
            value = feats[1] * feats[2]
            for g in range(groups):
                lanes = slice(g * LANES, (g + 1) * LANES)
                gate[source, g, pl.ds(start, rows), :] = feats[0][:, lanes]
                prod[source, g, pl.ds(start, rows), :] = value[:, lanes]

        for g in range(groups):
            lanes = slice(g * LANES, (g + 1) * LANES)
            factor = [consts[0, m, :, lanes] for m in range(modes)]

            def step(i, state):
                v = prod[source, g, pl.ds(i, SUBLANES, stride=steps), :]
                return tuple(f * q + v for f, q in zip(factor, state))

            zero = jnp.zeros((SUBLANES, LANES), jnp.float32)
            state = lax.fori_loop(0, steps, step, (zero,) * modes, unroll=4)
            for m in range(modes):
                st[source, m, :, lanes] = state[m]
        sub_decay = jnp.exp(-dec_ref[:, columns(z)] * steps)
        e = jnp.zeros((modes, C), jnp.float32)
        for c in range(SUBLANES):
            e = sub_decay * e + st[source, :, c, :]
        seg[source] = e
        allseg[x, source] = e
        for o in range(1, X):
            seg_copy(source, o).start()

    def compute(s):
        @pl.loop(0, 2 if s else 1)
        def _(side):
            source = z - s + 2 * s * side

            @pl.when(jnp.logical_and(source >= 0, source < Z))
            def _():
                for mask in held(len(bits) - 1) if bits else ():
                    for g in range(G):
                        tok_arrived(source, slot(mask + bits[-1]), g)
                multiply(source)
                tail_copy(source).start()

        @pl.loop(0, 2 if s else 1)
        def _(side):
            source = z - s + 2 * s * side

            @pl.when(jnp.logical_and(source >= 0, source < Z))
            def _():
                tail_copy(source).wait_recv()

        @pl.loop(0, 3)
        def _(i):
            source = jnp.where(i == 0, z + s, jnp.where(i == 1, z - s + 1, 0))
            right = jnp.logical_and(i == 0, jnp.logical_and(s >= 1, z + s < Z))
            left = jnp.logical_and(i == 1, jnp.logical_and(s >= 1, z - s >= 0))
            first = jnp.logical_and(i == 2, z == s)

            @pl.when(jnp.logical_or(right, jnp.logical_or(left, first)))
            def _():
                local_filter(source)

    for g in range(G):
        for side in (0, 1):
            @pl.when(onward(side))
            def _():
                tok_line(side, z, g, own_piece(g)).start()
    for o in range(1, X):
        w_cross(z, o, w_ref.at[:, :, columns(z)]).start()
    for s in range(Z - 1, 0, -1):
        for side in (0, 1):
            @pl.when(exists(1 - side, s))
            def _():
                w_line(z + s if side == 0 else z - s).start()

    dec = dec_ref[:, columns(z)]
    gain = res_ref[:, columns(z)] * jnp.sqrt(2.0 * dec)
    decay = jnp.exp(-dec)
    for m in range(modes):
        consts[0, m] = jnp.broadcast_to(decay[m : m + 1], (SUBLANES, C))
        consts[1, m] = jnp.broadcast_to(gain[m : m + 1], (SUBLANES, C))

    levels = len(bits)
    if bits:
        for g in range(G):
            start_level(0, 0, g)
    if Z > 1:
        for g in range(G):
            take_line(1, g)
    for level in range(1, levels):
        for s in range(min(2, Z)):
            for g in range(G):
                start_level(level, s, g)
    for s in range(Z - 1, 0, -1):
        take_w(s)
    own_tok.wait()
    own_w.wait()
    if Z > 2:
        for g in range(G):
            take_line(2, g)
        for level in range(1, levels):
            for g in range(G):
                start_level(level, 2, g)
    for source in range(Z):
        for o in range(1, X):
            w_arrived(source, (x + o) % X)
    for s in range(min(2, Z)):
        compute(s)
    for s in range(3, Z):
        compute_first = s - 1
        for g in range(G):
            take_line(s, g)
            if g:
                for level in range(1, levels):
                    start_level(level, s, g - 1)
        for level in range(1, levels):
            start_level(level, s, G - 1)
        compute(compute_first)
    if Z > 2:
        compute(Z - 1)

    for source in range(Z):
        for o in range(1, X):
            q = (x + o) % X
            remote(
                seg.at[source], allseg.at[q, source], seg_send.at[source, o], seg_recv.at[q, source],
                (z * X + q, t),
            ).wait_recv()
            seg_copy(source, o).wait_send()
    seg_decay = jnp.exp(-dec * L)
    sub_decay = jnp.exp(-dec * steps)
    carry = jnp.zeros((modes, C), jnp.float32)
    for s in range(Z):
        mine = jnp.zeros((modes, C), jnp.float32)
        for q in range(X):
            mine = jnp.where(x == q, carry, mine)
            carry = seg_decay * carry + allseg[q, s]
        seg[s] = mine

    def out_copy(s):
        return remote(
            outbuf.at[s], out_ref.at[:, columns(z)], out_send.at[s], out_recv.at[z], (s * X + x, t)
        )

    own_out = pltpu.make_async_copy(outbuf.at[z], out_ref.at[:, columns(z)], own_sem.at[0])

    @pl.loop(0, Z)
    def _(k):
        s = (z + 1 + k) % Z
        e = seg[s]
        for c in range(SUBLANES):
            now = st[s, :, c, :]
            st[s, :, c, :] = e
            e = sub_decay * e + now
        for g in range(groups):
            lanes = slice(g * LANES, (g + 1) * LANES)
            direct = jnp.broadcast_to(skip_ref[:, columns(z)][:, lanes], (SUBLANES, LANES))

            def step(i, state):
                at = pl.ds(i, SUBLANES, stride=steps)
                v = prod[s, g, at, :]
                state = tuple(consts[0, m, :, lanes] * q + v for m, q in enumerate(state))
                parts = [consts[1, m, :, lanes] * q for m, q in enumerate(state)]
                parts.append(direct * v)
                while len(parts) > 1:
                    parts = [a + b for a, b in zip(parts[::2], parts[1::2])] + (
                        [parts[-1]] if len(parts) % 2 else []
                    )
                gate[s, g, at, :] = gate[s, g, at, :] * parts[0]
                return state

            lax.fori_loop(0, steps, step, tuple(st[s, m, :, lanes] for m in range(modes)), unroll=4)
            outbuf[s, :, lanes] = gate[s, g].astype(outbuf.dtype)

        @pl.when(s != z)
        def _():
            out_copy(s).start()

        @pl.when(s == z)
        def _():
            own_out.start()

    for side in (0, 1):
        for s in range(Z - 1):
            @pl.when(jnp.logical_and(exists(side, s), onward(side)))
            def _():
                source = at_distance(side, s)
                for g in range(G):
                    tok_line(side, source, g, piece(source, t, g)).wait_send()
    for source in range(Z):
        for o in range(1, X):
            w_cross(source, o, w.at[:, source, x]).wait_send()
        for level in range(levels):
            for g in range(G):
                for copy in tp_copies(level, source, g, False):
                    copy.wait_send()
        tail_copy(source).wait_send()
    own_out.wait()
    for o in range(1, Z):
        q = (z + o) % Z
        w_line(q).wait_send()
        out_copy(q).wait_send()
        remote(
            outbuf.at[q], out_ref.at[:, columns(q)], out_send.at[q], out_recv.at[q], (q * X + x, t)
        ).wait_recv()


def line_length(count, token_bytes, weight_bytes, channels):
    best = None
    for Z in range(1, count):
        if count % Z or channels % (Z * LANES):
            continue
        cost = token_bytes * Z + 2 * weight_bytes // Z
        if best is None or cost < best[0]:
            best = (cost, Z)
    return best[1]


def per_device(tokens, in_weight, short_filter, decay_rates, residues, skip_gain):
    count, T = lax.axis_size("ctx"), lax.axis_size("tp")
    R, D = tokens.shape
    depth, branches, channels = in_weight.shape
    modes = decay_rates.shape[0]
    Z = line_length(count, R * T * D, depth * count * branches * channels, channels)
    X = count // Z
    C = channels // Z
    L = R * T
    G = max(1, min(PIECES, R // TAIL))
    levels = max(1, (T - 1).bit_length())
    dma = pltpu.SemaphoreType.DMA
    hbm = pl.BlockSpec(memory_space=pl.ANY)
    vmem = pl.BlockSpec(memory_space=pltpu.VMEM)
    f32, bf16 = jnp.float32, jnp.bfloat16
    return pl.pallas_call(
        functools.partial(fused_kernel, Z, X, T),
        out_shape=jax.ShapeDtypeStruct((L, channels), bf16),
        in_specs=[hbm, hbm, vmem, vmem, vmem, vmem],
        out_specs=hbm,
        scratch_shapes=[
            pltpu.VMEM((Z, T, R, D), bf16),
            pltpu.VMEM((branches, Z, X, depth, C), bf16),
            pltpu.VMEM((Z, branches, L + SUBLANES, C), f32),
            pltpu.VMEM((Z, branches, TAIL, C), bf16),
            pltpu.VMEM((Z, branches, TAIL, C), bf16),
            pltpu.VMEM((Z, C // LANES, L, LANES), f32),
            pltpu.VMEM((Z, C // LANES, L, LANES), f32),
            pltpu.VMEM((2, modes, SUBLANES, C), f32),
            pltpu.VMEM((Z, modes, SUBLANES, C), f32),
            pltpu.VMEM((Z, modes, C), f32),
            pltpu.VMEM((X, Z, modes, C), f32),
            pltpu.VMEM((Z, L, C), bf16),
            dma((Z, T, G)), dma((Z, X)), dma((2, Z, G)), dma((levels, Z, T, G)), dma((Z,)), dma((Z, X)),
            dma((Z,)), dma((Z,)), dma((Z, X)), dma((X, Z)), dma((Z,)), dma((Z,)), dma((2,)),
        ],
        compiler_params=pltpu.CompilerParams(
            collective_id=0, has_side_effects=True, vmem_limit_bytes=VMEM_BYTES
        ),
        name="project_and_filter",
    )(tokens, in_weight.transpose(1, 0, 2), short_filter, decay_rates, residues, skip_gain[None])


def solution(mesh):
    in_specs = (
        P(("ctx", "tp"), None),
        P("ctx", None, "tp"),
        P(None, None, "tp"),
        P(None, "tp"),
        P(None, "tp"),
        P("tp"),
    )
    return jax.shard_map(
        per_device, mesh=mesh, in_specs=in_specs, out_specs=P("ctx", "tp"), check_vma=False
    )
```

```python
import functools

import jax
import jax.numpy as jnp
from jax import lax
from jax.experimental import pallas as pl
from jax.experimental.pallas import tpu as pltpu
from jax.sharding import PartitionSpec as P

MESH = pl.DeviceIdType.MESH
VMEM_BYTES = 60 * 1024 * 1024
SUBLANES = 8
TAIL = 16
PIECES = 4
LANES = 128


def flipped(index, bit):
    return index + bit - 2 * bit * ((index // bit) % 2)


def fused_kernel(Z, X, T, tok_ref, w_ref, filt_ref, dec_ref, res_ref, skip_ref, out_ref,
                 tok, w, wid, tail, halo, prod, gate, consts, st, seg, allseg, outbuf,
                 tok_recv, w_recv, send_z, send_t, send_wz, send_wx,
                 halo_send, halo_recv, seg_send, seg_recv, out_send, out_recv, own_sem):
    ctx, t = lax.axis_index("ctx"), lax.axis_index("tp")
    z, x = ctx // X, ctx % X
    R = tok.shape[2]
    G = send_z.shape[2]
    part = R // G
    branches, depth = w.shape[0], w.shape[3]
    groups, L = prod.shape[1], prod.shape[2]
    C = groups * LANES
    modes, lags = dec_ref.shape[0], filt_ref.shape[1]
    steps = L // SUBLANES
    bits = []
    bit = T // 2
    while bit:
        bits.append(bit)
        bit //= 2

    def columns(index):
        return pl.ds(pl.multiple_of(index * C, LANES), C)

    own_tok = pltpu.make_async_copy(tok_ref, tok.at[z, t], own_sem.at[0])
    own_w = pltpu.make_async_copy(w_ref.at[:, :, columns(z)], w.at[:, z, x], own_sem.at[1])
    own_tok.start()
    own_w.start()

    barrier = pltpu.get_barrier_semaphore()
    for o in range(1, Z):
        pl.semaphore_signal(barrier, inc=1, device_id=(((z + o) % Z) * X + x, t), device_id_type=MESH)
    for o in range(1, X):
        pl.semaphore_signal(barrier, inc=1, device_id=(z * X + (x + o) % X, t), device_id_type=MESH)
    for bit in bits:
        pl.semaphore_signal(barrier, inc=1, device_id=(ctx, flipped(t, bit)), device_id_type=MESH)
    pl.semaphore_wait(barrier, Z - 1 + X - 1 + len(bits))

    def remote(src, dst, send, recv, device):
        return pltpu.make_async_remote_copy(
            src_ref=src, dst_ref=dst, send_sem=send, recv_sem=recv, device_id=device, device_id_type=MESH
        )

    def exists(side, s):
        return z - s >= 0 if side == 0 else z + s < Z

    def onward(side):
        return z + 1 < Z if side == 0 else z >= 1

    def at_distance(side, s):
        return z - s if side == 0 else z + s

    def piece(source, q, g):
        return tok.at[source, q, pl.ds(g * part, part)]

    def own_piece(g):
        return tok_ref.at[pl.ds(g * part, part)]

    def tok_line(side, source, g, src):
        to = z + 1 if side == 0 else z - 1
        return remote(
            src, piece(source, t, g), send_z.at[side, source, g], tok_recv.at[source, t, g], (to * X + x, t)
        )

    def held(level):
        masks = [0]
        for bit in bits[:level]:
            masks = masks + [m + bit for m in masks]
        return masks

    def slot(mask):
        index = t
        for bit in bits:
            if mask & bit:
                index = flipped(index, bit)
        return index

    def tp_copies(level, source, g, own):
        copies = []
        for mask in held(level):
            q = slot(mask)
            src = own_piece(g) if own and mask == 0 else piece(source, q, g)
            copies.append(
                remote(
                    src, piece(source, q, g), send_t.at[level, source, mask, g], tok_recv.at[source, q, g],
                    (ctx, flipped(t, bits[level])),
                )
            )
        return copies

    def tok_arrived(source, q, g):
        ref = piece(source, q, g)
        remote(ref, ref, own_sem.at[0], tok_recv.at[source, q, g], (ctx, t)).wait_recv()

    def w_line(target):
        return remote(
            w_ref.at[:, :, columns(target)], w.at[:, z, x], send_wz.at[target], w_recv.at[z, x], (target * X + x, t)
        )

    def w_cross(source, o, src):
        return remote(
            src, w.at[:, source, x], send_wx.at[source, o], w_recv.at[source, x], (z * X + (x + o) % X, t)
        )

    def w_arrived(source, q):
        ref = w.at[:, source, q]
        remote(ref, ref, own_sem.at[0], w_recv.at[source, q], (ctx, t)).wait_recv()

    def tail_copy(source):
        return remote(
            tail.at[source], halo.at[source], halo_send.at[source], halo_recv.at[source], (z * X + (x + 1) % X, t)
        )

    def seg_copy(source, o):
        return remote(
            seg.at[source], allseg.at[x, source], seg_send.at[source, o], seg_recv.at[x, source],
            (z * X + (x + o) % X, t),
        )

    def take_line(s, g):
        for side in (0, 1):
            @pl.when(exists(side, s))
            def _():
                source = at_distance(side, s)
                tok_arrived(source, t, g)

                @pl.when(onward(side))
                def _():
                    tok_line(side, source, g, piece(source, t, g)).start()

                if bits:
                    for copy in tp_copies(0, source, g, False):
                        copy.start()

    def start_level(level, s, g):
        for side in (0, 1) if s else (0,):
            def act():
                source = at_distance(side, s)
                if level > 0:
                    for mask in held(level - 1):
                        tok_arrived(source, slot(mask + bits[level - 1]), g)
                for copy in tp_copies(level, source, g, s == 0):
                    copy.start()

            pl.when(exists(side, s))(act)

    def take_w(s):
        for side in (0, 1):
            @pl.when(exists(side, s))
            def _():
                source = at_distance(side, s)
                w_arrived(source, x)
                for o in range(1, X):
                    w_cross(source, o, w.at[:, source, x]).start()

    def multiply(source):
        a = tok.at[source].reshape(T * R, Z * X * depth)

        @pl.loop(0, branches)
        def _(j):
            b = w.at[j].reshape(Z * X * depth, C)
            value = jnp.dot(a[...], b[...], preferred_element_type=jnp.float32).astype(jnp.bfloat16)
            tail[source, j] = value[L - TAIL :]
            wid[source, j, SUBLANES:] = value.astype(jnp.float32)

    rows = 32

    def local_filter(source):
        before = jnp.where(x == 0, source - 1, source)

        @pl.loop(0, branches)
        def _(j):
            last = halo[jnp.maximum(before, 0), j].astype(jnp.float32)
            wid[source, j, 0:SUBLANES] = jnp.where(before >= 0, last[TAIL - SUBLANES :], 0.0)

        @pl.loop(0, L // rows)
        def _(r):
            start = pl.multiple_of(r * rows, rows)
            feats = []
            for j in range(branches):
                block = wid[source, j, pl.ds(start, rows + SUBLANES)]
                total = None
                for o in range(lags):
                    term = filt_ref[j, o : o + 1, columns(z)] * block[SUBLANES - o : SUBLANES - o + rows]
                    total = term if total is None else total + term
                feats.append(total)
            value = feats[1] * feats[2]
            for g in range(groups):
                lanes = slice(g * LANES, (g + 1) * LANES)
                gate[source, g, pl.ds(start, rows), :] = feats[0][:, lanes]
                prod[source, g, pl.ds(start, rows), :] = value[:, lanes]

        for g in range(groups):
            lanes = slice(g * LANES, (g + 1) * LANES)
            factor = [consts[0, m, :, lanes] for m in range(modes)]

            def step(i, state):
                v = prod[source, g, pl.ds(i, SUBLANES, stride=steps), :]
                return tuple(f * q + v for f, q in zip(factor, state))

            zero = jnp.zeros((SUBLANES, LANES), jnp.float32)
            state = lax.fori_loop(0, steps, step, (zero,) * modes, unroll=4)
            for m in range(modes):
                st[source, m, :, lanes] = state[m]
        sub_decay = jnp.exp(-dec_ref[:, columns(z)] * steps)
        e = jnp.zeros((modes, C), jnp.float32)
        for c in range(SUBLANES):
            e = sub_decay * e + st[source, :, c, :]
        seg[source] = e
        allseg[x, source] = e
        for o in range(1, X):
            seg_copy(source, o).start()

    def compute(s):
        @pl.loop(0, 2 if s else 1)
        def _(side):
            source = z - s + 2 * s * side

            @pl.when(jnp.logical_and(source >= 0, source < Z))
            def _():
                for mask in held(len(bits) - 1) if bits else ():
                    for g in range(G):
                        tok_arrived(source, slot(mask + bits[-1]), g)
                multiply(source)
                tail_copy(source).start()

        @pl.loop(0, 2 if s else 1)
        def _(side):
            source = z - s + 2 * s * side

            @pl.when(jnp.logical_and(source >= 0, source < Z))
            def _():
                tail_copy(source).wait_recv()

        @pl.loop(0, 3)
        def _(i):
            source = jnp.where(i == 0, z + s, jnp.where(i == 1, z - s + 1, 0))
            right = jnp.logical_and(i == 0, jnp.logical_and(s >= 1, z + s < Z))
            left = jnp.logical_and(i == 1, jnp.logical_and(s >= 1, z - s >= 0))
            first = jnp.logical_and(i == 2, z == s)

            @pl.when(jnp.logical_or(right, jnp.logical_or(left, first)))
            def _():
                local_filter(source)

    for g in range(G):
        for side in (0, 1):
            @pl.when(onward(side))
            def _():
                tok_line(side, z, g, own_piece(g)).start()
    for o in range(1, X):
        w_cross(z, o, w_ref.at[:, :, columns(z)]).start()
    for s in range(Z - 1, 0, -1):
        for side in (0, 1):
            @pl.when(exists(1 - side, s))
            def _():
                w_line(z + s if side == 0 else z - s).start()

    dec = dec_ref[:, columns(z)]
    gain = res_ref[:, columns(z)] * jnp.sqrt(2.0 * dec)
    decay = jnp.exp(-dec)
    for m in range(modes):
        consts[0, m] = jnp.broadcast_to(decay[m : m + 1], (SUBLANES, C))
        consts[1, m] = jnp.broadcast_to(gain[m : m + 1], (SUBLANES, C))

    levels = len(bits)
    if bits:
        for g in range(G):
            start_level(0, 0, g)
    if Z > 1:
        for g in range(G):
            take_line(1, g)
    for level in range(1, levels):
        for s in range(min(2, Z)):
            for g in range(G):
                start_level(level, s, g)
    for s in range(Z - 1, 0, -1):
        take_w(s)
    own_tok.wait()
    own_w.wait()
    if Z > 2:
        for g in range(G):
            take_line(2, g)
        for level in range(1, levels):
            for g in range(G):
                start_level(level, 2, g)
    for source in range(Z):
        for o in range(1, X):
            w_arrived(source, (x + o) % X)
    compute(0)
    if Z <= 3:
        compute(1)
    for s in range(3, Z):
        compute_first = s - 1
        for g in range(G):
            take_line(s, g)
            if g:
                for level in range(1, levels):
                    start_level(level, s, g - 1)
        for level in range(1, levels):
            start_level(level, s, G - 1)
        if s == 3:
            compute(1)
        compute(compute_first)
    if Z > 2:
        compute(Z - 1)

    for source in range(Z):
        for o in range(1, X):
            q = (x + o) % X
            remote(
                seg.at[source], allseg.at[q, source], seg_send.at[source, o], seg_recv.at[q, source],
                (z * X + q, t),
            ).wait_recv()
            seg_copy(source, o).wait_send()
    seg_decay = jnp.exp(-dec * L)
    sub_decay = jnp.exp(-dec * steps)
    carry = jnp.zeros((modes, C), jnp.float32)
    for s in range(Z):
        mine = jnp.zeros((modes, C), jnp.float32)
        for q in range(X):
            mine = jnp.where(x == q, carry, mine)
            carry = seg_decay * carry + allseg[q, s]
        seg[s] = mine

    def out_copy(s):
        return remote(
            outbuf.at[s], out_ref.at[:, columns(z)], out_send.at[s], out_recv.at[z], (s * X + x, t)
        )

    own_out = pltpu.make_async_copy(outbuf.at[z], out_ref.at[:, columns(z)], own_sem.at[0])

    @pl.loop(0, Z)
    def _(k):
        s = jnp.where(2 * z < Z, Z - 1 - k, k)
        e = seg[s]
        for c in range(SUBLANES):
            now = st[s, :, c, :]
            st[s, :, c, :] = e
            e = sub_decay * e + now
        for g in range(groups):
            lanes = slice(g * LANES, (g + 1) * LANES)
            direct = jnp.broadcast_to(skip_ref[:, columns(z)][:, lanes], (SUBLANES, LANES))

            def step(i, state):
                at = pl.ds(i, SUBLANES, stride=steps)
                v = prod[s, g, at, :]
                state = tuple(consts[0, m, :, lanes] * q + v for m, q in enumerate(state))
                parts = [consts[1, m, :, lanes] * q for m, q in enumerate(state)]
                parts.append(direct * v)
                while len(parts) > 1:
                    parts = [a + b for a, b in zip(parts[::2], parts[1::2])] + (
                        [parts[-1]] if len(parts) % 2 else []
                    )
                gate[s, g, at, :] = gate[s, g, at, :] * parts[0]
                return state

            lax.fori_loop(0, steps, step, tuple(st[s, m, :, lanes] for m in range(modes)), unroll=4)
            outbuf[s, :, lanes] = gate[s, g].astype(outbuf.dtype)

        @pl.when(s != z)
        def _():
            out_copy(s).start()

        @pl.when(s == z)
        def _():
            own_out.start()

    for side in (0, 1):
        for s in range(Z - 1):
            @pl.when(jnp.logical_and(exists(side, s), onward(side)))
            def _():
                source = at_distance(side, s)
                for g in range(G):
                    tok_line(side, source, g, piece(source, t, g)).wait_send()
    for source in range(Z):
        for o in range(1, X):
            w_cross(source, o, w.at[:, source, x]).wait_send()
        for level in range(levels):
            for g in range(G):
                for copy in tp_copies(level, source, g, False):
                    copy.wait_send()
        tail_copy(source).wait_send()
    own_out.wait()
    for o in range(1, Z):
        q = (z + o) % Z
        w_line(q).wait_send()
        out_copy(q).wait_send()
        remote(
            outbuf.at[q], out_ref.at[:, columns(q)], out_send.at[q], out_recv.at[q], (q * X + x, t)
        ).wait_recv()


def line_length(count, token_bytes, weight_bytes, channels):
    best = None
    for Z in range(1, count):
        if count % Z or channels % (Z * LANES):
            continue
        cost = token_bytes * Z + 2 * weight_bytes // Z
        if best is None or cost < best[0]:
            best = (cost, Z)
    return best[1]


def per_device(tokens, in_weight, short_filter, decay_rates, residues, skip_gain):
    count, T = lax.axis_size("ctx"), lax.axis_size("tp")
    R, D = tokens.shape
    depth, branches, channels = in_weight.shape
    modes = decay_rates.shape[0]
    Z = line_length(count, R * T * D, depth * count * branches * channels, channels)
    X = count // Z
    C = channels // Z
    L = R * T
    G = max(1, min(PIECES, R // TAIL))
    levels = max(1, (T - 1).bit_length())
    dma = pltpu.SemaphoreType.DMA
    hbm = pl.BlockSpec(memory_space=pl.ANY)
    vmem = pl.BlockSpec(memory_space=pltpu.VMEM)
    f32, bf16 = jnp.float32, jnp.bfloat16
    return pl.pallas_call(
        functools.partial(fused_kernel, Z, X, T),
        out_shape=jax.ShapeDtypeStruct((L, channels), bf16),
        in_specs=[hbm, hbm, vmem, vmem, vmem, vmem],
        out_specs=hbm,
        scratch_shapes=[
            pltpu.VMEM((Z, T, R, D), bf16),
            pltpu.VMEM((branches, Z, X, depth, C), bf16),
            pltpu.VMEM((Z, branches, L + SUBLANES, C), f32),
            pltpu.VMEM((Z, branches, TAIL, C), bf16),
            pltpu.VMEM((Z, branches, TAIL, C), bf16),
            pltpu.VMEM((Z, C // LANES, L, LANES), f32),
            pltpu.VMEM((Z, C // LANES, L, LANES), f32),
            pltpu.VMEM((2, modes, SUBLANES, C), f32),
            pltpu.VMEM((Z, modes, SUBLANES, C), f32),
            pltpu.VMEM((Z, modes, C), f32),
            pltpu.VMEM((X, Z, modes, C), f32),
            pltpu.VMEM((Z, L, C), bf16),
            dma((Z, T, G)), dma((Z, X)), dma((2, Z, G)), dma((levels, Z, T, G)), dma((Z,)), dma((Z, X)),
            dma((Z,)), dma((Z,)), dma((Z, X)), dma((X, Z)), dma((Z,)), dma((Z,)), dma((2,)),
        ],
        compiler_params=pltpu.CompilerParams(
            collective_id=0, has_side_effects=True, vmem_limit_bytes=VMEM_BYTES
        ),
        name="project_and_filter",
    )(tokens, in_weight.transpose(1, 0, 2), short_filter, decay_rates, residues, skip_gain[None])


def solution(mesh):
    in_specs = (
        P(("ctx", "tp"), None),
        P("ctx", None, "tp"),
        P(None, None, "tp"),
        P(None, "tp"),
        P(None, "tp"),
        P("tp"),
    )
    return jax.shard_map(
        per_device, mesh=mesh, in_specs=in_specs, out_specs=P("ctx", "tp"), check_vma=False
    )
```
